32 devices in a mesh: day: 2 (over x), chan: 16 (over z, y, core).
Axes of the slice: x: 2, y: 2, z: 4, core: 2. Of those that a mesh axis runs over, the one named last changes fastest.
Arguments:
- file_blocks: bfloat16 [224, 16, 1024], P(('day', 'chan')), parts along dimension 0, may hold values from -132 to 132
- block_target: int32 [224], P(('day', 'chan')), parts along dimension 0, may hold values from -1 to 63, as said below
Outputs:
- correlations: bfloat16 [512, 64, 144], P(('day', 'chan')), parts along dimension 0
The draws below stay inside these ranges and needn't reach their ends.
There are 2 independent parts, one for each index of `day`. The reference program is written for one: setup_inputs(seed, part) draws one part's arguments, and reference() takes and returns one part's arrays. A program takes and returns all parts, laid end to end along the dimension named above; each array names one. Nothing has to cross between parts.
Inputs may be any that keep to these rules, and one draw needn't show every extreme that they name: `block_target`: -1 marks an empty slot and a device's filled slots come first; each device holds 1 to 7 blocks. A value v names window v % 4 of channel owner v // 4; every such pair appears exactly once. Devices 2k and 2k+1 together hold exactly the 8 blocks of owners 2k and 2k+1; in every draw some device holds all 4 blocks of its neighbour owner in the pair.
All inputs are finite; a program needn't handle non-finite values.
Results may differ from the reference program's by a relative error of at most 0.0073.
Values may be sent and summed in bfloat16 or wider, within the bound.
No kernel may reach another device: no remote copies, remote signals or barrier semaphores. Data moves between devices by JAX's collectives and lax.ppermute only.
A program may use at most 64 MiB of HBM per device.

```python
import math
import jax
import jax.numpy as jnp
from jax import lax

CH_DEV = 16
NW = 4
WIN = 1024
BANDS = 128
BAND_LO = 16
SMOOTH = 4
LAGS = 64
SLOTS = 7
N_CHAN = 16


def pair_layout(key):
    pairs = N_CHAN // 2
    items = 2 * NW
    keys = jax.random.split(jax.random.fold_in(key, 41), 5)
    pair_ids = jnp.arange(pairs, dtype=jnp.int32)
    spread = jax.random.randint(keys[0], (pairs,), 0, NW).astype(jnp.int32)
    forced = jax.random.randint(keys[1], (), 0, pairs).astype(jnp.int32)
    spread = jnp.where(pair_ids == forced, NW - 1, spread)
    flips = jax.random.randint(keys[2], (pairs,), 0, 2).astype(jnp.int32)
    first_count = jnp.where(flips == 1, NW + spread, NW - spread)
    orders = jax.vmap(lambda sub_key: jax.random.permutation(sub_key, items))(jax.random.split(keys[3], pairs)).astype(jnp.int32)
    chosen = (1 - flips) * NW + jax.random.randint(keys[4], (pairs,), 0, NW).astype(jnp.int32)
    spots = jnp.where(flips == 0, 0, items - 1).astype(jnp.int32)

    def adjust(order_row, picked, place):
        found = jnp.argmax(order_row == picked)
        moved = order_row.at[found].set(order_row[place])
        return moved.at[place].set(picked)
    adjusted = jax.vmap(adjust)(orders, chosen, spots)
    orders = jnp.where((pair_ids == forced)[:, None], adjusted, orders)
    slot_ids = jnp.arange(SLOTS, dtype=jnp.int32)
    first_index = jnp.broadcast_to(slot_ids[None, :], (pairs, SLOTS))
    first_valid = slot_ids[None, :] < first_count[:, None]
    second_index = first_count[:, None] + slot_ids[None, :]
    second_valid = slot_ids[None, :] < (items - first_count)[:, None]
    index_all = jnp.stack([first_index, second_index], axis=1)
    valid_all = jnp.stack([first_valid, second_valid], axis=1)
    clipped = jnp.clip(index_all, 0, items - 1).reshape(pairs, 2 * SLOTS)
    picked_items = jnp.take_along_axis(orders, clipped, axis=1).reshape(pairs, 2, SLOTS)
    targets = (2 * pair_ids[:, None, None] + picked_items // NW) * NW + picked_items % NW
    targets = jnp.where(valid_all, targets, -1)
    return targets.reshape(-1).astype(jnp.int32)


def draw_block_target(key, part):
    return pair_layout(key)


def draw_file_blocks(key, part):
    keys = jax.random.split(jax.random.fold_in(key, 23), 5)
    rows = N_CHAN * SLOTS
    scales = jnp.exp(jax.random.uniform(keys[0], (rows, CH_DEV, 1), jnp.float32, 0.0, math.log(10.0)))
    tones = jax.random.randint(keys[1], (rows, CH_DEV, 1), BAND_LO, BAND_LO + BANDS).astype(jnp.int32)
    heights = jax.random.uniform(keys[2], (rows, CH_DEV, 1), jnp.float32, 1.0, 4.0)
    phases = jax.random.uniform(keys[3], (rows, CH_DEV, 1), jnp.float32, -math.pi, math.pi)
    times = jnp.arange(WIN, dtype=jnp.int32)
    angle = 2.0 * math.pi / WIN * (tones * times[None, None, :] % WIN).astype(jnp.float32) + phases
    noise = jnp.clip(jax.random.normal(keys[4], (rows, CH_DEV, WIN), jnp.float32), -5.0, 5.0)
    values = scales * (noise + heights * jnp.sin(angle))
    return values.astype(jnp.bfloat16)


def setup_inputs(seed: int = 0, part: int = 0) -> dict:
    key_of = jax.random.split(jax.random.key(seed), 3)
    part_splits = jax.random.split(jax.random.fold_in(key_of[2], part), 3)
    file_blocks = draw_file_blocks(jax.random.fold_in(jax.random.fold_in(key_of[2], part), 71), part)
    block_target = draw_block_target(jax.random.fold_in(jax.random.fold_in(key_of[2], part), 71), part)
    return {"file_blocks": file_blocks, "block_target": block_target}


def fourier_table(samples, bands, band_low):
    times = jnp.arange(samples, dtype=jnp.int32)
    bins = band_low + jnp.arange(bands, dtype=jnp.int32)
    phase = times[:, None] * bins[None, :] % samples
    angle = 2.0 * math.pi / samples * phase.astype(jnp.float32)
    taper = 0.5 - 0.5 * jnp.cos(2.0 * math.pi / samples * times.astype(jnp.float32))
    rows = jnp.concatenate([taper[:, None] * jnp.cos(angle), -taper[:, None] * jnp.sin(angle)], axis=1)
    return rows.astype(jnp.bfloat16)

def lag_table(samples, bands, band_low, lags, windows):
    bins = band_low + jnp.arange(bands, dtype=jnp.int32)
    delays = jnp.arange(lags, dtype=jnp.int32) - lags // 2
    phase = bins[:, None] * delays[None, :] % samples
    angle = 2.0 * math.pi / samples * phase.astype(jnp.float32)
    weight = 1.0 / math.sqrt(windows * bands)
    rows = jnp.stack([jnp.cos(angle) * weight, -jnp.sin(angle) * weight])
    return rows.astype(jnp.bfloat16)

def whiten(spectra, bands, smooth):
    real_part = spectra[..., :bands]
    imag_part = spectra[..., bands:]
    power = real_part * real_part + imag_part * imag_part
    widths = [(0, 0)] * (power.ndim - 1) + [(smooth, smooth)]
    padded = jnp.pad(power, widths)
    nearby = padded[..., 0:bands]
    for shift_bins in range(1, 2 * smooth + 1):
        nearby = nearby + padded[..., shift_bins:shift_bins + bands]
    level = nearby / (2 * smooth + 1) + 0.25 * lax.optimization_barrier(jnp.mean(power, axis=-1, keepdims=True)) + 1e-05
    factor = 1.0 / jnp.sqrt(level)
    return jnp.concatenate([real_part * factor, imag_part * factor], axis=-1).astype(jnp.bfloat16)

def pair_block(own_block, other_block, lag_rows, bands):
    windows = own_block.shape[0]
    own_wide = own_block.astype(jnp.float32)
    other_wide = other_block.astype(jnp.float32)
    own_split = own_wide.reshape(windows, own_wide.shape[1], 2, bands)
    other_split = other_wide.reshape(windows, other_wide.shape[1], 2, bands)
    same_part = jnp.einsum('wicb,wjcb->bij', own_split, other_split)
    turned = jnp.einsum('wib,wjb->bij', own_split[:, :, 1], other_split[:, :, 0]) - jnp.einsum('wib,wjb->bij', own_split[:, :, 0], other_split[:, :, 1])
    cross = jnp.stack([same_part, turned]).astype(jnp.bfloat16)
    result = jnp.einsum('pbij,pbt->itj', cross.astype(jnp.float32), lag_rows.astype(jnp.float32))
    return result.astype(jnp.bfloat16)

def reference(file_blocks, block_target):
    transform = fourier_table(WIN, BANDS, BAND_LO)
    lag_rows = lag_table(WIN, BANDS, BAND_LO, LAGS, NW)
    total = N_CHAN * NW
    filled = block_target >= 0
    where_to = jnp.where(filled, block_target, total).astype(jnp.int32)
    slot_of = jnp.zeros((total + 1,), jnp.int32).at[where_to].set(jnp.arange(block_target.shape[0], dtype=jnp.int32))
    records = file_blocks[slot_of[:total]]
    records = records.reshape(N_CHAN, NW, CH_DEV, WIN).transpose(1, 0, 2, 3).reshape(NW * N_CHAN * CH_DEV, WIN)
    spectra = jnp.dot(records, transform, preferred_element_type=jnp.float32)
    spectra = spectra.reshape(NW, N_CHAN * CH_DEV, 2 * BANDS)
    whitened = whiten(spectra, BANDS, SMOOTH).reshape(NW, N_CHAN, CH_DEV, 2 * BANDS)
    half_cycle = N_CHAN // 2

    def per_owner(owner_index):
        own_block = lax.dynamic_index_in_dim(whitened, owner_index, 1, keepdims=False)

        def per_offset(offset):
            source = ((owner_index + offset) % N_CHAN).astype(jnp.int32)
            other_block = lax.dynamic_index_in_dim(whitened, source, 1, keepdims=False)
            return pair_block(own_block, other_block, lag_rows, BANDS)
        blocks = jax.vmap(per_offset)(jnp.arange(half_cycle + 1, dtype=jnp.int32))
        return blocks.transpose(1, 2, 0, 3).reshape(CH_DEV, LAGS, (half_cycle + 1) * CH_DEV)
    result = lax.map(per_owner, jnp.arange(N_CHAN, dtype=jnp.int32))
    return result.reshape(N_CHAN * CH_DEV, LAGS, (half_cycle + 1) * CH_DEV)
```

```python
import functools
import math

import jax
import jax.numpy as jnp
import numpy as np
from jax import lax
from jax.experimental import pallas as pl
from jax.experimental.pallas import tpu as pltpu
from jax.sharding import PartitionSpec as P

NW = 4
BANDS = 128
BAND_LO = 16
SMOOTH = 4
LAGS = 64


def fourier_table(samples, bands, band_low):
    times = np.arange(samples, dtype=np.int32)
    bins = band_low + np.arange(bands, dtype=np.int32)
    phase = times[:, None] * bins[None, :] % samples
    step = np.float32(2.0 * math.pi / samples)
    angle = step * phase.astype(np.float32)
    half = np.float32(0.5)
    taper = half - half * np.cos(step * times.astype(np.float32))
    rows = np.concatenate([taper[:, None] * np.cos(angle), -taper[:, None] * np.sin(angle)], axis=1)
    return rows.astype(jnp.bfloat16)


def lag_table(samples, bands, band_low, lags, windows):
    bins = band_low + np.arange(bands, dtype=np.int32)
    delays = np.arange(lags, dtype=np.int32) - lags // 2
    phase = bins[None, :] * delays[:, None] % samples
    angle = np.float32(2.0 * math.pi / samples) * phase.astype(np.float32)
    weight = np.float32(1.0 / math.sqrt(windows * bands))
    rows = np.stack([np.cos(angle) * weight, -np.sin(angle) * weight])
    return rows.astype(jnp.bfloat16).astype(np.float32)


def spectra_kernel(target_ref, blocks_ref, table_ref, out_ref):
    slots, channels, samples = blocks_ref.shape
    rows = blocks_ref[...].reshape(slots * channels, samples)
    spectra = jnp.dot(rows, table_ref[...], preferred_element_type=jnp.float32)
    real_part = spectra[:, :BANDS]
    imag_part = spectra[:, BANDS:]
    power = real_part * real_part + imag_part * imag_part
    lane = lax.broadcasted_iota(jnp.int32, power.shape, 1)

    def shifted(value, by):
        moved = pltpu.roll(value, by % BANDS, 1)
        inside = lane >= by if by > 0 else lane < BANDS + by
        return jnp.where(inside, moved, 0.0)

    nearby = power
    for by in range(1, SMOOTH + 1):
        nearby = nearby + shifted(power, by) + shifted(power, -by)
    mean = jnp.sum(power, axis=-1, keepdims=True) / BANDS
    level = nearby / (2 * SMOOTH + 1) + 0.25 * mean + 1e-05
    factor = lax.rsqrt(level)
    whitened = jnp.concatenate([real_part * factor, imag_part * factor], axis=1).astype(jnp.bfloat16)
    out_ref[...] = jnp.zeros_like(out_ref)
    for slot in range(slots):
        target = target_ref[slot]

        @pl.when(target >= 0)
        def _():
            place = lax.rem(target, 2 * NW)
            out_ref[place] = whitened[slot * channels : (slot + 1) * channels]


def steer_kernel(core_ref, chip_ref, lag_ref, out_ref):
    channels = chip_ref.shape[1]
    core = core_ref[0]
    lag_cos = lag_ref[0]
    lag_sin = lag_ref[1]
    for window in range(NW):
        own = chip_ref[core * NW + window].astype(jnp.float32)
        for channel in range(channels):
            real_part = own[channel : channel + 1, :BANDS]
            imag_part = own[channel : channel + 1, BANDS:]
            first = lag_cos * real_part + lag_sin * imag_part
            second = lag_cos * imag_part - lag_sin * real_part
            out_ref[window, channel, :, :BANDS] = first.astype(jnp.bfloat16)
            out_ref[window, channel, :, BANDS:] = second.astype(jnp.bfloat16)


def product_kernel(order, core_ref, steer_ref, chip_ref, mine_ref, other_ref, out_ref, gathered):
    channels, lags, columns = out_ref.shape
    offsets = columns // channels
    core = core_ref[0]
    gathered[0:2] = chip_ref[...].reshape(gathered[0:2].shape)
    for step in range(len(order) // 2):
        low, high = order[2 * step], order[2 * step + 1]
        here = jnp.where(core == 0, low, high)
        there = jnp.where(core == 0, high, low)
        gathered[pl.ds(2 * here, 2)] = mine_ref[step].reshape(gathered[0:2].shape)
        gathered[pl.ds(2 * there, 2)] = other_ref[step].reshape(gathered[0:2].shape)
    total = None
    for window in range(NW):
        left = steer_ref[window].reshape(channels * lags, 2 * BANDS)
        right = gathered[pl.ds(core, offsets), window].reshape(columns, 2 * BANDS)
        part = lax.dot_general(
            left, right, (((1,), (1,)), ((), ())), preferred_element_type=jnp.float32
        )
        total = part if total is None else total + part
    out_ref[...] = total.astype(jnp.bfloat16).reshape(out_ref.shape)


def vmem(count):
    return [pl.BlockSpec(memory_space=pltpu.VMEM)] * count


def smem(count):
    return [pl.BlockSpec(memory_space=pltpu.SMEM)] * count


def shards(file_blocks, block_target):
    slot_count, channels, samples = file_blocks.shape
    devices = lax.axis_size("chan")
    chips = devices // 2
    half_cycle = devices // 2
    reach = (half_cycle + 1) // 2
    order = list(range(1, reach + 1, 2)) + list(range(reach - reach % 2, 0, -2))
    if len(order) % 2:
        order.append(order[-1])
    core = lax.rem(lax.axis_index("chan"), 2).astype(jnp.int32).reshape(1)
    transform = jnp.asarray(fourier_table(samples, BANDS, BAND_LO))
    lag_rows = jnp.asarray(lag_table(samples, BANDS, BAND_LO, LAGS, NW))

    def swap_cores(value):
        return lax.ppermute(value, "chan", [(s, s ^ 1) for s in range(devices)])

    def fetch(value, low, high):
        pairs = []
        for chip in range(chips):
            pairs.append(((chip + low) % chips * 2, chip * 2))
            pairs.append(((chip + high) % chips * 2 + 1, chip * 2 + 1))
        return lax.ppermute(value, "chan", pairs)

    held = pl.pallas_call(
        spectra_kernel,
        out_shape=jax.ShapeDtypeStruct((2 * NW, channels, 2 * BANDS), jnp.bfloat16),
        in_specs=smem(1) + vmem(2),
        out_specs=vmem(1)[0],
        compiler_params=pltpu.CompilerParams(vmem_limit_bytes=8 << 20),
        name="spectra",
    )(block_target, file_blocks, transform)
    chip_blocks = held + swap_cores(held)
    fetched = [
        fetch(chip_blocks, order[2 * step], order[2 * step + 1]) for step in range(len(order) // 2)
    ]
    steer = pl.pallas_call(
        steer_kernel,
        out_shape=jax.ShapeDtypeStruct((NW, channels, LAGS, 2 * BANDS), jnp.bfloat16),
        in_specs=smem(1) + vmem(2),
        out_specs=vmem(1)[0],
        compiler_params=pltpu.CompilerParams(vmem_limit_bytes=8 << 20),
        cost_estimate=pl.CostEstimate(flops=6 << 20, bytes_accessed=2 << 20, transcendentals=0),
        name="steer",
    )(core, chip_blocks, lag_rows)
    mine = jnp.stack(fetched)
    other = swap_cores(mine)
    columns = (half_cycle + 1) * channels
    return pl.pallas_call(
        functools.partial(product_kernel, order),
        out_shape=jax.ShapeDtypeStruct((channels, LAGS, columns), jnp.bfloat16),
        in_specs=smem(1) + vmem(4),
        out_specs=vmem(1)[0],
        scratch_shapes=[pltpu.VMEM((2 * (reach + 1), NW, channels, 2 * BANDS), jnp.bfloat16)],
        compiler_params=pltpu.CompilerParams(vmem_limit_bytes=32 << 20),
        name="product",
    )(core, steer, chip_blocks, mine, other)


def solution(mesh):
    return jax.shard_map(
        shards,
        mesh=mesh,
        in_specs=(P(("day", "chan"), None, None), P(("day", "chan"))),
        out_specs=P(("day", "chan"), None, None),
        check_vma=False,
    )
```

```python
import functools
import math

import jax
import jax.numpy as jnp
import numpy as np
from jax import lax
from jax.experimental import pallas as pl
from jax.experimental.pallas import tpu as pltpu
from jax.sharding import PartitionSpec as P

NW = 4
BANDS = 128
BAND_LO = 16
SMOOTH = 4
LAGS = 64
PIECES = 4


def fourier_table(samples, bands, band_low):
    times = np.arange(samples, dtype=np.int32)
    bins = band_low + np.arange(bands, dtype=np.int32)
    phase = times[:, None] * bins[None, :] % samples
    step = np.float32(2.0 * math.pi / samples)
    angle = step * phase.astype(np.float32)
    half = np.float32(0.5)
    taper = half - half * np.cos(step * times.astype(np.float32))
    rows = np.concatenate([taper[:, None] * np.cos(angle), -taper[:, None] * np.sin(angle)], axis=1)
    return rows.astype(jnp.bfloat16)


def lag_table(samples, bands, band_low, lags, windows):
    bins = band_low + np.arange(bands, dtype=np.int32)
    delays = np.arange(lags, dtype=np.int32) - lags // 2
    phase = bins[None, :] * delays[:, None] % samples
    angle = np.float32(2.0 * math.pi / samples) * phase.astype(np.float32)
    weight = np.float32(1.0 / math.sqrt(windows * bands))
    rows = np.stack([np.cos(angle) * weight, -np.sin(angle) * weight])
    return rows.astype(jnp.bfloat16).astype(np.float32)


def spectra_kernel(target_hbm, blocks_hbm, table_hbm, out_ref, target_ref, blocks_ref, table_ref, sems):
    slots, channels, samples = blocks_ref.shape
    pieces = table_ref.shape[0]
    depth = samples // pieces
    copies = [
        pltpu.make_async_copy(blocks_hbm, blocks_ref, sems.at[0]),
        pltpu.make_async_copy(target_hbm, target_ref, sems.at[1]),
    ]
    for piece in range(pieces):
        copies.append(
            pltpu.make_async_copy(
                table_hbm.at[pl.ds(piece * depth, depth)], table_ref.at[piece], sems.at[2 + piece]
            )
        )
    for copy in copies:
        copy.start()
    out_ref[...] = jnp.zeros_like(out_ref)
    copies[0].wait()
    spectra = None
    for piece in range(pieces):
        copies[2 + piece].wait()
        rows = blocks_ref[:, :, piece * depth : (piece + 1) * depth].reshape(slots * channels, depth)
        part = jnp.dot(rows, table_ref[piece], preferred_element_type=jnp.float32)
        spectra = part if spectra is None else spectra + part
    real_part = spectra[:, :BANDS]
    imag_part = spectra[:, BANDS:]
    power = real_part * real_part + imag_part * imag_part
    lane = lax.broadcasted_iota(jnp.int32, power.shape, 1)

    def shifted(value, by):
        moved = pltpu.roll(value, by % BANDS, 1)
        inside = lane >= by if by > 0 else lane < BANDS + by
        return jnp.where(inside, moved, 0.0)

    nearby = power
    for by in range(1, SMOOTH + 1):
        nearby = nearby + shifted(power, by) + shifted(power, -by)
    mean = jnp.sum(power, axis=-1, keepdims=True) / BANDS
    level = nearby / (2 * SMOOTH + 1) + 0.25 * mean + 1e-05
    factor = lax.rsqrt(level)
    whitened = jnp.concatenate([real_part * factor, imag_part * factor], axis=1).astype(jnp.bfloat16)
    copies[1].wait()
    for slot in range(slots):
        target = target_ref[slot]

        @pl.when(target >= 0)
        def _():
            place = lax.rem(target, 2 * NW)
            out_ref[place] = whitened[slot * channels : (slot + 1) * channels]


def steer_kernel(core_ref, chip_ref, lag_ref, out_ref):
    channels = chip_ref.shape[1]
    core = core_ref[0]
    lag_cos = lag_ref[0]
    lag_sin = lag_ref[1]
    for window in range(NW):
        own = chip_ref[core * NW + window].astype(jnp.float32)
        low = window * 2 * BANDS
        for channel in range(channels):
            real_part = own[channel : channel + 1, :BANDS]
            imag_part = own[channel : channel + 1, BANDS:]
            first = lag_cos * real_part + lag_sin * imag_part
            second = lag_cos * imag_part - lag_sin * real_part
            out_ref[channel, :, low : low + BANDS] = first.astype(jnp.bfloat16)
            out_ref[channel, :, low + BANDS : low + 2 * BANDS] = second.astype(jnp.bfloat16)


def product_kernel(order, core_ref, steer_ref, chip_ref, mine_ref, other_ref, out_ref, gathered):
    channels, lags, columns = out_ref.shape
    offsets = columns // channels
    width = 2 * BANDS
    core = core_ref[0]

    def place(chip, blocks):
        for owner in range(2):
            for window in range(NW):
                gathered[2 * chip + owner, :, window * width : (window + 1) * width] = blocks[
                    owner * NW + window
                ]

    place(0, chip_ref)
    for step in range(len(order) // 2):
        low, high = order[2 * step], order[2 * step + 1]
        place(jnp.where(core == 0, low, high), mine_ref.at[step])
        place(jnp.where(core == 0, high, low), other_ref.at[step])
    right = gathered[pl.ds(core, offsets)].reshape(columns, NW * width)
    left = steer_ref[...].reshape(channels * lags, NW * width)
    total = lax.dot_general(
        left, right, (((1,), (1,)), ((), ())), preferred_element_type=jnp.float32
    )
    out_ref[...] = total.astype(jnp.bfloat16).reshape(out_ref.shape)


def vmem(count):
    return [pl.BlockSpec(memory_space=pltpu.VMEM)] * count


def smem(count):
    return [pl.BlockSpec(memory_space=pltpu.SMEM)] * count


def hbm(count):
    return [pl.BlockSpec(memory_space=pltpu.HBM)] * count


def shards(file_blocks, block_target):
    slot_count, channels, samples = file_blocks.shape
    devices = lax.axis_size("chan")
    chips = devices // 2
    half_cycle = devices // 2
    reach = (half_cycle + 1) // 2
    order = list(range(1, reach + 1, 2)) + list(range(reach - reach % 2, 0, -2))
    if len(order) % 2:
        order.append(order[-1])
    core = lax.rem(lax.axis_index("chan"), 2).astype(jnp.int32).reshape(1)
    transform = jnp.asarray(fourier_table(samples, BANDS, BAND_LO))
    lag_rows = jnp.asarray(lag_table(samples, BANDS, BAND_LO, LAGS, NW))

    def swap_cores(value):
        return lax.ppermute(value, "chan", [(s, s ^ 1) for s in range(devices)])

    def fetch(value, low, high):
        pairs = []
        for chip in range(chips):
            pairs.append(((chip + low) % chips * 2, chip * 2))
            pairs.append(((chip + high) % chips * 2 + 1, chip * 2 + 1))
        return lax.ppermute(value, "chan", pairs)

    held = pl.pallas_call(
        spectra_kernel,
        out_shape=jax.ShapeDtypeStruct((2 * NW, channels, 2 * BANDS), jnp.bfloat16),
        in_specs=hbm(3),
        out_specs=vmem(1)[0],
        scratch_shapes=[
            pltpu.SMEM(block_target.shape, jnp.int32),
            pltpu.VMEM(file_blocks.shape, jnp.bfloat16),
            pltpu.VMEM((PIECES, samples // PIECES, 2 * BANDS), jnp.bfloat16),
            pltpu.SemaphoreType.DMA((2 + PIECES,)),
        ],
        compiler_params=pltpu.CompilerParams(vmem_limit_bytes=8 << 20),
        name="spectra",
    )(*[pltpu.with_memory_space_constraint(v, pltpu.HBM) for v in (block_target, file_blocks, transform)])
    chip_blocks = held + swap_cores(held)
    fetched = [
        fetch(chip_blocks, order[2 * step], order[2 * step + 1]) for step in range(len(order) // 2)
    ]
    steer = pl.pallas_call(
        steer_kernel,
        out_shape=jax.ShapeDtypeStruct((channels, LAGS, NW * 2 * BANDS), jnp.bfloat16),
        in_specs=smem(1) + vmem(2),
        out_specs=vmem(1)[0],
        compiler_params=pltpu.CompilerParams(vmem_limit_bytes=8 << 20),
        cost_estimate=pl.CostEstimate(flops=6 << 20, bytes_accessed=2 << 20, transcendentals=0),
        name="steer",
    )(core, chip_blocks, lag_rows)
    mine, steer = lax.optimization_barrier((jnp.stack(fetched), steer))
    other = swap_cores(mine)
    columns = (half_cycle + 1) * channels
    return pl.pallas_call(
        functools.partial(product_kernel, order),
        out_shape=jax.ShapeDtypeStruct((channels, LAGS, columns), jnp.bfloat16),
        in_specs=smem(1) + vmem(4),
        out_specs=vmem(1)[0],
        scratch_shapes=[pltpu.VMEM((2 * (reach + 1), channels, NW * 2 * BANDS), jnp.bfloat16)],
        compiler_params=pltpu.CompilerParams(vmem_limit_bytes=32 << 20),
        name="product",
    )(core, steer, chip_blocks, mine, other)


def solution(mesh):
    return jax.shard_map(
        shards,
        mesh=mesh,
        in_specs=(P(("day", "chan"), None, None), P(("day", "chan"))),
        out_specs=P(("day", "chan"), None, None),
        check_vma=False,
    )
```

```python
import functools
import math

import jax
import jax.numpy as jnp
import numpy as np
from jax import lax
from jax.experimental import pallas as pl
from jax.experimental.pallas import tpu as pltpu
from jax.sharding import PartitionSpec as P

NW = 4
BANDS = 128
BAND_LO = 16
SMOOTH = 4
LAGS = 64
PIECES = 4


def fourier_table(samples, bands, band_low):
    times = np.arange(samples, dtype=np.int32)
    bins = band_low + np.arange(bands, dtype=np.int32)
    phase = times[:, None] * bins[None, :] % samples
    step = np.float32(2.0 * math.pi / samples)
    angle = step * phase.astype(np.float32)
    half = np.float32(0.5)
    taper = half - half * np.cos(step * times.astype(np.float32))
    rows = np.concatenate([taper[:, None] * np.cos(angle), -taper[:, None] * np.sin(angle)], axis=1)
    return rows.astype(jnp.bfloat16)


def sum_table(bands, smooth):
    bins = np.arange(bands)
    near = np.abs(bins[:, None] - bins[None, :]) <= smooth
    rows = np.concatenate([near, np.ones_like(near)], axis=1)
    return np.concatenate([rows, rows]).astype(jnp.bfloat16)


def lag_table(samples, bands, band_low, lags, windows):
    bins = band_low + np.arange(bands, dtype=np.int32)
    delays = np.arange(lags, dtype=np.int32) - lags // 2
    phase = bins[None, :] * delays[:, None] % samples
    angle = np.float32(2.0 * math.pi / samples) * phase.astype(np.float32)
    weight = np.float32(1.0 / math.sqrt(windows * bands))
    rows = np.stack([np.cos(angle) * weight, -np.sin(angle) * weight])
    return rows.astype(jnp.bfloat16).astype(np.float32)


def load_kernel(target_hbm, blocks_hbm, table_hbm, target_ref, blocks_ref, table_ref, sems):
    pairs = [(target_hbm, target_ref), (blocks_hbm, blocks_ref), (table_hbm, table_ref)]
    copies = [pltpu.make_async_copy(here, there, sems.at[at]) for at, (here, there) in enumerate(pairs)]
    for copy in copies:
        copy.start()
    for copy in copies:
        copy.wait()


def spectra_kernel(
    target_ref, far_target_ref, blocks_ref, far_blocks_ref, table_ref, out_ref, target, far_target, sems
):
    slots, channels, samples = blocks_ref.shape
    places = 2 * NW
    copies = [
        pltpu.make_async_copy(target_ref, target, sems.at[0]),
        pltpu.make_async_copy(far_target_ref, far_target, sems.at[1]),
    ]
    for copy in copies:
        copy.start()
    rows = jnp.concatenate(
        [ref[...].reshape(slots * channels, samples) for ref in (blocks_ref, far_blocks_ref)]
    )
    spectra = jnp.dot(rows, table_ref[:samples], preferred_element_type=jnp.float32)
    real_part = spectra[:, :BANDS]
    imag_part = spectra[:, BANDS:]
    power = real_part * real_part + imag_part * imag_part
    high = power.astype(jnp.bfloat16)
    low = (power - high.astype(jnp.float32)).astype(jnp.bfloat16)
    sums = jnp.dot(
        jnp.concatenate([high, low], axis=1), table_ref[samples:], preferred_element_type=jnp.float32
    )
    level = sums[:, :BANDS] * (1.0 / (2 * SMOOTH + 1)) + sums[:, BANDS:] * (0.25 / BANDS) + 1e-05
    factor = lax.rsqrt(level)
    real_part = (real_part * factor).astype(jnp.bfloat16)
    imag_part = (imag_part * factor).astype(jnp.bfloat16)
    for copy in copies:
        copy.wait()
    first = lax.rem(target[0], places)
    for slot in reversed(range(2 * slots)):
        value = target[slot] if slot < slots else far_target[slot - slots]
        place = jnp.where(value >= 0, lax.rem(value, places), first)
        span = slice(slot * channels, (slot + 1) * channels)
        out_ref[place, :, :BANDS] = real_part[span]
        out_ref[place, :, BANDS:] = imag_part[span]


def steer_kernel(core_ref, chip_ref, lag_ref, out_ref):
    channels = chip_ref.shape[1]
    core = core_ref[0]
    lag_cos = lag_ref[0]
    lag_sin = lag_ref[1]
    for window in range(NW):
        own = chip_ref[core * NW + window].astype(jnp.float32)
        low = window * 2 * BANDS
        for channel in range(channels):
            real_part = own[channel : channel + 1, :BANDS]
            imag_part = own[channel : channel + 1, BANDS:]
            first = lag_cos * real_part + lag_sin * imag_part
            second = lag_cos * imag_part - lag_sin * real_part
            out_ref[channel, :, low : low + BANDS] = first.astype(jnp.bfloat16)
            out_ref[channel, :, low + BANDS : low + 2 * BANDS] = second.astype(jnp.bfloat16)


def product_kernel(
    order, core_ref, steer_ref, chip_ref, mine_ref, other_ref, out_hbm, gathered, out_ref, sems
):
    channels, lags, columns = out_ref.shape
    offsets = columns // channels
    width = 2 * BANDS
    core = core_ref[0]

    def place(chip, blocks):
        for owner in range(2):
            for window in range(NW):
                gathered[2 * chip + owner, :, window * width : (window + 1) * width] = blocks[
                    owner * NW + window
                ]

    place(0, chip_ref)
    for step in range(len(order) // 2):
        low, high = order[2 * step], order[2 * step + 1]
        place(jnp.where(core == 0, low, high), mine_ref.at[step])
        place(jnp.where(core == 0, high, low), other_ref.at[step])
    right = gathered[pl.ds(core, offsets)].reshape(columns, NW * width)
    left = steer_ref[...].reshape(channels * lags, NW * width)
    total = lax.dot_general(
        left, right, (((1,), (1,)), ((), ())), preferred_element_type=jnp.float32
    )
    count = channels // PIECES
    copies = []
    for piece in range(PIECES):
        span = slice(piece * count * lags, (piece + 1) * count * lags)
        part = slice(piece * count, (piece + 1) * count)
        out_ref[part] = total[span].astype(jnp.bfloat16).reshape(count, lags, columns)
        copies.append(pltpu.make_async_copy(out_ref.at[part], out_hbm.at[part], sems.at[piece]))
        copies[-1].start()
    for copy in copies:
        copy.wait()


def vmem(count):
    return [pl.BlockSpec(memory_space=pltpu.VMEM)] * count


def smem(count):
    return [pl.BlockSpec(memory_space=pltpu.SMEM)] * count


def hbm(count):
    return [pl.BlockSpec(memory_space=pltpu.HBM)] * count


def shards(file_blocks, block_target):
    slot_count, channels, samples = file_blocks.shape
    devices = lax.axis_size("chan")
    chips = devices // 2
    half_cycle = devices // 2
    reach = (half_cycle + 1) // 2
    order = list(range(1, reach + 1, 2)) + list(range(reach - reach % 2, 0, -2))
    if len(order) % 2:
        order.append(order[-1])
    core = lax.rem(lax.axis_index("chan"), 2).astype(jnp.int32).reshape(1)
    transform = jnp.asarray(
        np.concatenate([fourier_table(samples, BANDS, BAND_LO), sum_table(BANDS, SMOOTH)])
    )
    lag_rows = jnp.asarray(lag_table(samples, BANDS, BAND_LO, LAGS, NW))

    def swap_cores(value):
        return lax.ppermute(value, "chan", [(s, s ^ 1) for s in range(devices)])

    def fetch(value, low, high):
        pairs = []
        for chip in range(chips):
            pairs.append(((chip + low) % chips * 2, chip * 2))
            pairs.append(((chip + high) % chips * 2 + 1, chip * 2 + 1))
        return lax.ppermute(value, "chan", pairs)

    far_target = swap_cores(block_target)
    far_blocks = swap_cores(file_blocks)
    inputs = (block_target, file_blocks, transform)
    target, blocks, table = pl.pallas_call(
        load_kernel,
        out_shape=[jax.ShapeDtypeStruct(v.shape, v.dtype) for v in inputs],
        in_specs=hbm(3),
        out_specs=vmem(3),
        scratch_shapes=[pltpu.SemaphoreType.DMA((3,))],
        compiler_params=pltpu.CompilerParams(vmem_limit_bytes=8 << 20),
        cost_estimate=pl.CostEstimate(flops=1 << 20, bytes_accessed=1 << 20, transcendentals=0),
        name="load",
    )(*[pltpu.with_memory_space_constraint(v, pltpu.HBM) for v in inputs])
    chip_blocks = pl.pallas_call(
        spectra_kernel,
        out_shape=jax.ShapeDtypeStruct((2 * NW, channels, 2 * BANDS), jnp.bfloat16),
        in_specs=vmem(5),
        out_specs=vmem(1)[0],
        scratch_shapes=[
            pltpu.SMEM(block_target.shape, jnp.int32),
            pltpu.SMEM(block_target.shape, jnp.int32),
            pltpu.SemaphoreType.DMA((2,)),
        ],
        compiler_params=pltpu.CompilerParams(vmem_limit_bytes=8 << 20),
        name="spectra",
    )(target, far_target, blocks, far_blocks, table)
    fetched = [
        fetch(chip_blocks, order[2 * step], order[2 * step + 1]) for step in range(len(order) // 2)
    ]
    steer = pl.pallas_call(
        steer_kernel,
        out_shape=jax.ShapeDtypeStruct((channels, LAGS, NW * 2 * BANDS), jnp.bfloat16),
        in_specs=smem(1) + vmem(2),
        out_specs=vmem(1)[0],
        compiler_params=pltpu.CompilerParams(vmem_limit_bytes=8 << 20),
        cost_estimate=pl.CostEstimate(flops=6 << 20, bytes_accessed=2 << 20, transcendentals=0),
        name="steer",
    )(core, chip_blocks, lag_rows)
    mine, steer = lax.optimization_barrier((jnp.stack(fetched), steer))
    other = swap_cores(mine)
    columns = (half_cycle + 1) * channels
    return pl.pallas_call(
        functools.partial(product_kernel, order),
        out_shape=jax.ShapeDtypeStruct((channels, LAGS, columns), jnp.bfloat16),
        in_specs=smem(1) + vmem(4),
        out_specs=hbm(1)[0],
        scratch_shapes=[
            pltpu.VMEM((2 * (reach + 1), channels, NW * 2 * BANDS), jnp.bfloat16),
            pltpu.VMEM((channels, LAGS, columns), jnp.bfloat16),
            pltpu.SemaphoreType.DMA((PIECES,)),
        ],
        compiler_params=pltpu.CompilerParams(vmem_limit_bytes=32 << 20),
        name="product",
    )(core, steer, chip_blocks, mine, other)


def solution(mesh):
    return jax.shard_map(
        shards,
        mesh=mesh,
        in_specs=(P(("day", "chan"), None, None), P(("day", "chan"))),
        out_specs=P(("day", "chan"), None, None),
        check_vma=False,
    )
```

```python
import functools
import math
import random

import jax
import jax.numpy as jnp
import numpy as np
from jax import lax
from jax.experimental import pallas as pl
from jax.experimental.pallas import tpu as pltpu
from jax.sharding import PartitionSpec as P

NW = 4
BANDS = 128
BAND_LO = 16
SMOOTH = 4
LAGS = 64
PIECES = 4
PLAN_SEED = 4034


def fourier_table(samples, bands, band_low):
    times = np.arange(samples, dtype=np.int32)
    bins = band_low + np.arange(bands, dtype=np.int32)
    phase = times[:, None] * bins[None, :] % samples
    step = np.float32(2.0 * math.pi / samples)
    angle = step * phase.astype(np.float32)
    half = np.float32(0.5)
    taper = half - half * np.cos(step * times.astype(np.float32))
    rows = np.concatenate([taper[:, None] * np.cos(angle), -taper[:, None] * np.sin(angle)], axis=1)
    return rows.astype(jnp.bfloat16)


def sum_table(bands, smooth):
    bins = np.arange(bands)
    near = np.abs(bins[:, None] - bins[None, :]) <= smooth
    rows = np.concatenate([near, np.ones_like(near)], axis=1)
    return np.concatenate([rows, rows]).astype(jnp.bfloat16)


def lag_table(samples, bands, band_low, lags, windows):
    bins = band_low + np.arange(bands, dtype=np.int32)
    delays = np.arange(lags, dtype=np.int32) - lags // 2
    phase = bins[None, :] * delays[:, None] % samples
    angle = np.float32(2.0 * math.pi / samples) * phase.astype(np.float32)
    weight = np.float32(1.0 / math.sqrt(windows * bands))
    rows = np.stack([np.cos(angle) * weight, -np.sin(angle) * weight])
    return rows.astype(jnp.bfloat16).astype(np.float32)


def load_kernel(target_hbm, blocks_hbm, table_hbm, target_ref, blocks_ref, table_ref, sems):
    pairs = [(target_hbm, target_ref), (blocks_hbm, blocks_ref), (table_hbm, table_ref)]
    copies = [pltpu.make_async_copy(here, there, sems.at[at]) for at, (here, there) in enumerate(pairs)]
    for copy in copies:
        copy.start()
    for copy in copies:
        copy.wait()


def spectra_kernel(
    target_ref, far_target_ref, blocks_ref, far_blocks_ref, table_ref, out_ref, target, far_target, sems
):
    slots, channels, samples = blocks_ref.shape
    places = 2 * NW
    copies = [
        pltpu.make_async_copy(target_ref, target, sems.at[0]),
        pltpu.make_async_copy(far_target_ref, far_target, sems.at[1]),
    ]
    for copy in copies:
        copy.start()
    rows = jnp.concatenate(
        [ref[...].reshape(slots * channels, samples) for ref in (blocks_ref, far_blocks_ref)]
    )
    spectra = jnp.dot(rows, table_ref[:samples], preferred_element_type=jnp.float32)
    real_part = spectra[:, :BANDS]
    imag_part = spectra[:, BANDS:]
    power = real_part * real_part + imag_part * imag_part
    high = power.astype(jnp.bfloat16)
    low = (power - high.astype(jnp.float32)).astype(jnp.bfloat16)
    sums = jnp.dot(
        jnp.concatenate([high, low], axis=1), table_ref[samples:], preferred_element_type=jnp.float32
    )
    level = sums[:, :BANDS] * (1.0 / (2 * SMOOTH + 1)) + sums[:, BANDS:] * (0.25 / BANDS) + 1e-05
    factor = lax.rsqrt(level)
    real_part = (real_part * factor).astype(jnp.bfloat16)
    imag_part = (imag_part * factor).astype(jnp.bfloat16)
    for copy in copies:
        copy.wait()
    first = lax.rem(target[0], places)
    for slot in reversed(range(2 * slots)):
        value = target[slot] if slot < slots else far_target[slot - slots]
        place = jnp.where(value >= 0, lax.rem(value, places), first)
        span = slice(slot * channels, (slot + 1) * channels)
        out_ref[place, :, :BANDS] = real_part[span]
        out_ref[place, :, BANDS:] = imag_part[span]


def steer_kernel(device_ref, chip_ref, lag_ref, out_ref):
    channels = chip_ref.shape[1]
    core = lax.rem(device_ref[0], 2)
    lag_cos = lag_ref[0]
    lag_sin = lag_ref[1]
    for window in range(NW):
        own = chip_ref[core * NW + window].astype(jnp.float32)
        low = window * 2 * BANDS
        for channel in range(channels):
            real_part = own[channel : channel + 1, :BANDS]
            imag_part = own[channel : channel + 1, BANDS:]
            first = lag_cos * real_part + lag_sin * imag_part
            second = lag_cos * imag_part - lag_sin * real_part
            out_ref[channel, :, low : low + BANDS] = first.astype(jnp.bfloat16)
            out_ref[channel, :, low + BANDS : low + 2 * BANDS] = second.astype(jnp.bfloat16)


def entry(table, index):
    bits = max(table).bit_length()
    count = 30 // bits
    word = jnp.int32(0)
    for start in range(0, len(table), count):
        packed = sum(value << bits * at for at, value in enumerate(table[start : start + count]))
        word = jnp.where(index >= start, jnp.int32(packed), word)
    shift = bits * lax.rem(index, count)
    return lax.shift_right_logical(word, shift) & ((1 << bits) - 1)


def product_kernel(
    ahead, device_ref, steer_ref, chip_ref, mine_ref, other_ref, out_hbm, gathered, out_ref, sems
):
    channels, lags, columns = out_ref.shape
    offsets = columns // channels
    width = 2 * BANDS
    device = device_ref[0]
    core = lax.rem(device, 2)
    own_chip = lax.div(device, 2)

    def place(chip, blocks):
        for owner in range(2):
            for window in range(NW):
                gathered[2 * chip + owner, :, window * width : (window + 1) * width] = blocks[
                    owner * NW + window
                ]

    place(0, chip_ref)
    for step in range(mine_ref.shape[0]):
        even = entry(ahead[2 * step], own_chip)
        odd = entry(ahead[2 * step + 1], own_chip)
        place(jnp.where(core == 0, even, odd), mine_ref.at[step])
        place(jnp.where(core == 0, odd, even), other_ref.at[step])
    right = gathered[pl.ds(core, offsets)].reshape(columns, NW * width)
    left = steer_ref[...].reshape(channels * lags, NW * width)
    total = lax.dot_general(
        left, right, (((1,), (1,)), ((), ())), preferred_element_type=jnp.float32
    )
    count = channels // PIECES
    copies = []
    for piece in range(PIECES):
        span = slice(piece * count * lags, (piece + 1) * count * lags)
        part = slice(piece * count, (piece + 1) * count)
        out_ref[part] = total[span].astype(jnp.bfloat16).reshape(count, lags, columns)
        copies.append(pltpu.make_async_copy(out_ref.at[part], out_hbm.at[part], sems.at[piece]))
        copies[-1].start()
    for copy in copies:
        copy.wait()


def fetch_plan(chips, reach, seed):
    draw = random.Random(seed)
    left = [[(chip + offset) % chips for offset in range(1, reach + 1)] for chip in range(chips)]
    plan = []
    for _ in range(reach):
        taker = {}

        def claim(chip, seen):
            sources = list(left[chip])
            draw.shuffle(sources)
            for source in sources:
                if source not in seen:
                    seen.add(source)
                    if source not in taker or claim(taker[source], seen):
                        taker[source] = chip
                        return True
            return False

        chip_order = list(range(chips))
        draw.shuffle(chip_order)
        for chip in chip_order:
            claim(chip, set())
        matching = [0] * chips
        for source, chip in taker.items():
            matching[chip] = source
            left[chip].remove(source)
        plan.append(matching)
    return plan


def vmem(count):
    return [pl.BlockSpec(memory_space=pltpu.VMEM)] * count


def smem(count):
    return [pl.BlockSpec(memory_space=pltpu.SMEM)] * count


def hbm(count):
    return [pl.BlockSpec(memory_space=pltpu.HBM)] * count


def shards(file_blocks, block_target):
    slot_count, channels, samples = file_blocks.shape
    devices = lax.axis_size("chan")
    chips = devices // 2
    half_cycle = devices // 2
    reach = (half_cycle + 1) // 2
    plan = fetch_plan(chips, reach, PLAN_SEED)
    if reach % 2:
        plan.append(plan[-1])
    steps = len(plan) // 2
    device = lax.axis_index("chan").astype(jnp.int32).reshape(1)
    ahead = [[(row[chip] - chip) % chips for chip in range(chips)] for row in plan]
    transform = jnp.asarray(
        np.concatenate([fourier_table(samples, BANDS, BAND_LO), sum_table(BANDS, SMOOTH)])
    )
    lag_rows = jnp.asarray(lag_table(samples, BANDS, BAND_LO, LAGS, NW))

    def swap_cores(value):
        return lax.ppermute(value, "chan", [(s, s ^ 1) for s in range(devices)])

    def fetch(value, step):
        pairs = []
        for chip in range(chips):
            for side in range(2):
                pairs.append((plan[2 * step + side][chip] * 2 + side, chip * 2 + side))
        return lax.ppermute(value, "chan", pairs)

    far_target = swap_cores(block_target)
    far_blocks = swap_cores(file_blocks)
    inputs = (block_target, file_blocks, transform)
    target, blocks, table = pl.pallas_call(
        load_kernel,
        out_shape=[jax.ShapeDtypeStruct(v.shape, v.dtype) for v in inputs],
        in_specs=hbm(3),
        out_specs=vmem(3),
        scratch_shapes=[pltpu.SemaphoreType.DMA((3,))],
        compiler_params=pltpu.CompilerParams(vmem_limit_bytes=8 << 20),
        cost_estimate=pl.CostEstimate(flops=1 << 20, bytes_accessed=1 << 20, transcendentals=0),
        name="load",
    )(*[pltpu.with_memory_space_constraint(v, pltpu.HBM) for v in inputs])
    chip_blocks = pl.pallas_call(
        spectra_kernel,
        out_shape=jax.ShapeDtypeStruct((2 * NW, channels, 2 * BANDS), jnp.bfloat16),
        in_specs=vmem(5),
        out_specs=vmem(1)[0],
        scratch_shapes=[
            pltpu.SMEM(block_target.shape, jnp.int32),
            pltpu.SMEM(block_target.shape, jnp.int32),
            pltpu.SemaphoreType.DMA((2,)),
        ],
        compiler_params=pltpu.CompilerParams(vmem_limit_bytes=8 << 20),
        name="spectra",
    )(target, far_target, blocks, far_blocks, table)
    fetched = [fetch(chip_blocks, step) for step in range(steps)]
    steer = pl.pallas_call(
        steer_kernel,
        out_shape=jax.ShapeDtypeStruct((channels, LAGS, NW * 2 * BANDS), jnp.bfloat16),
        in_specs=smem(1) + vmem(2),
        out_specs=vmem(1)[0],
        compiler_params=pltpu.CompilerParams(vmem_limit_bytes=8 << 20),
        cost_estimate=pl.CostEstimate(flops=6 << 20, bytes_accessed=2 << 20, transcendentals=0),
        name="steer",
    )(device, chip_blocks, lag_rows)
    mine, steer = lax.optimization_barrier((jnp.stack(fetched), steer))
    other = swap_cores(mine)
    columns = (half_cycle + 1) * channels
    return pl.pallas_call(
        functools.partial(product_kernel, ahead),
        out_shape=jax.ShapeDtypeStruct((channels, LAGS, columns), jnp.bfloat16),
        in_specs=smem(1) + vmem(4),
        out_specs=hbm(1)[0],
        scratch_shapes=[
            pltpu.VMEM((2 * (reach + 1), channels, NW * 2 * BANDS), jnp.bfloat16),
            pltpu.VMEM((channels, LAGS, columns), jnp.bfloat16),
            pltpu.SemaphoreType.DMA((PIECES,)),
        ],
        compiler_params=pltpu.CompilerParams(vmem_limit_bytes=32 << 20),
        name="product",
    )(device, steer, chip_blocks, mine, other)


def solution(mesh):
    return jax.shard_map(
        shards,
        mesh=mesh,
        in_specs=(P(("day", "chan"), None, None), P(("day", "chan"))),
        out_specs=P(("day", "chan"), None, None),
        check_vma=False,
    )
```

```python
import functools
import math
import random

import jax
import jax.numpy as jnp
import numpy as np
from jax import lax
from jax.experimental import pallas as pl
from jax.experimental.pallas import tpu as pltpu
from jax.sharding import PartitionSpec as P

NW = 4
BANDS = 128
BAND_LO = 16
SMOOTH = 4
LAGS = 64
PIECES = 4
PLAN_SEED = 4034
ROUTES = (
    (5, 3, 7, 11, 9, 6, 15, 8, 12, 10, 13, 0, 14, 2, 1, 4),
    (7, 9, 8, 4, 10, 13, 11, 12, 14, 0, 15, 3, 1, 5, 6, 2),
)


def fourier_table(samples, bands, band_low):
    times = np.arange(samples, dtype=np.int32)
    bins = band_low + np.arange(bands, dtype=np.int32)
    phase = times[:, None] * bins[None, :] % samples
    step = np.float32(2.0 * math.pi / samples)
    angle = step * phase.astype(np.float32)
    half = np.float32(0.5)
    taper = half - half * np.cos(step * times.astype(np.float32))
    rows = np.concatenate([taper[:, None] * np.cos(angle), -taper[:, None] * np.sin(angle)], axis=1)
    return rows.astype(jnp.bfloat16)


def sum_table(bands, smooth):
    bins = np.arange(bands)
    near = np.abs(bins[:, None] - bins[None, :]) <= smooth
    rows = np.concatenate([near, np.ones_like(near)], axis=1)
    return np.concatenate([rows, rows]).astype(jnp.bfloat16)


def lag_table(samples, bands, band_low, lags, windows):
    bins = band_low + np.arange(bands, dtype=np.int32)
    delays = np.arange(lags, dtype=np.int32) - lags // 2
    phase = bins[None, :] * delays[:, None] % samples
    angle = np.float32(2.0 * math.pi / samples) * phase.astype(np.float32)
    weight = np.float32(1.0 / math.sqrt(windows * bands))
    rows = np.stack([np.cos(angle) * weight, -np.sin(angle) * weight])
    return rows.astype(jnp.bfloat16).astype(np.float32)


def load_kernel(target_hbm, blocks_hbm, table_hbm, target_ref, blocks_ref, table_ref, sems):
    pairs = [(target_hbm, target_ref), (blocks_hbm, blocks_ref), (table_hbm, table_ref)]
    copies = [pltpu.make_async_copy(here, there, sems.at[at]) for at, (here, there) in enumerate(pairs)]
    for copy in copies:
        copy.start()
    for copy in copies:
        copy.wait()


def spectra_kernel(
    target_ref, far_target_ref, blocks_ref, far_blocks_ref, table_ref, out_ref, target, far_target, sems
):
    slots, channels, samples = blocks_ref.shape
    places = 2 * NW
    copies = [
        pltpu.make_async_copy(target_ref, target, sems.at[0]),
        pltpu.make_async_copy(far_target_ref, far_target, sems.at[1]),
    ]
    for copy in copies:
        copy.start()
    rows = jnp.concatenate(
        [ref[...].reshape(slots * channels, samples) for ref in (blocks_ref, far_blocks_ref)]
    )
    spectra = jnp.dot(rows, table_ref[:samples], preferred_element_type=jnp.float32)
    real_part = spectra[:, :BANDS]
    imag_part = spectra[:, BANDS:]
    power = real_part * real_part + imag_part * imag_part
    high = power.astype(jnp.bfloat16)
    low = (power - high.astype(jnp.float32)).astype(jnp.bfloat16)
    sums = jnp.dot(
        jnp.concatenate([high, low], axis=1), table_ref[samples:], preferred_element_type=jnp.float32
    )
    level = sums[:, :BANDS] * (1.0 / (2 * SMOOTH + 1)) + sums[:, BANDS:] * (0.25 / BANDS) + 1e-05
    factor = lax.rsqrt(level)
    real_part = (real_part * factor).astype(jnp.bfloat16)
    imag_part = (imag_part * factor).astype(jnp.bfloat16)
    for copy in copies:
        copy.wait()
    first = lax.rem(target[0], places)
    for slot in reversed(range(2 * slots)):
        value = target[slot] if slot < slots else far_target[slot - slots]
        place = jnp.where(value >= 0, lax.rem(value, places), first)
        span = slice(slot * channels, (slot + 1) * channels)
        out_ref[place, :, :BANDS] = real_part[span]
        out_ref[place, :, BANDS:] = imag_part[span]


def steer_kernel(device_ref, chip_ref, lag_ref, out_ref):
    channels = chip_ref.shape[1]
    core = lax.rem(device_ref[0], 2)
    lag_cos = lag_ref[0]
    lag_sin = lag_ref[1]
    for window in range(NW):
        own = chip_ref[core * NW + window].astype(jnp.float32)
        low = window * 2 * BANDS
        for channel in range(channels):
            real_part = own[channel : channel + 1, :BANDS]
            imag_part = own[channel : channel + 1, BANDS:]
            first = lag_cos * real_part + lag_sin * imag_part
            second = lag_cos * imag_part - lag_sin * real_part
            out_ref[channel, :, low : low + BANDS] = first.astype(jnp.bfloat16)
            out_ref[channel, :, low + BANDS : low + 2 * BANDS] = second.astype(jnp.bfloat16)


def entry(table, index):
    bits = max(table).bit_length()
    count = 30 // bits
    word = jnp.int32(0)
    for start in range(0, len(table), count):
        packed = sum(value << bits * at for at, value in enumerate(table[start : start + count]))
        word = jnp.where(index >= start, jnp.int32(packed), word)
    shift = bits * lax.rem(index, count)
    return lax.shift_right_logical(word, shift) & ((1 << bits) - 1)


def product_kernel(
    ahead, device_ref, steer_ref, chip_ref, mine_ref, other_ref, out_hbm, gathered, out_ref, sems
):
    channels, lags, columns = out_ref.shape
    offsets = columns // channels
    width = 2 * BANDS
    device = device_ref[0]
    core = lax.rem(device, 2)
    own_chip = lax.div(device, 2)

    def place(chip, blocks):
        for owner in range(2):
            for window in range(NW):
                gathered[2 * chip + owner, :, window * width : (window + 1) * width] = blocks[
                    owner * NW + window
                ]

    place(0, chip_ref)
    for step in range(mine_ref.shape[0]):
        even = entry(ahead[2 * step], own_chip)
        odd = entry(ahead[2 * step + 1], own_chip)
        place(jnp.where(core == 0, even, odd), mine_ref.at[step])
        place(jnp.where(core == 0, odd, even), other_ref.at[step])
    right = gathered[pl.ds(core, offsets)].reshape(columns, NW * width)
    left = steer_ref[...].reshape(channels * lags, NW * width)
    total = lax.dot_general(
        left, right, (((1,), (1,)), ((), ())), preferred_element_type=jnp.float32
    )
    count = channels // PIECES
    copies = []
    for piece in range(PIECES):
        span = slice(piece * count * lags, (piece + 1) * count * lags)
        part = slice(piece * count, (piece + 1) * count)
        out_ref[part] = total[span].astype(jnp.bfloat16).reshape(count, lags, columns)
        copies.append(pltpu.make_async_copy(out_ref.at[part], out_hbm.at[part], sems.at[piece]))
        copies[-1].start()
    for copy in copies:
        copy.wait()


def fetch_plan(chips, reach, seed):
    draw = random.Random(seed)
    left = [[(chip + offset) % chips for offset in range(1, reach + 1)] for chip in range(chips)]
    plan = []
    for _ in range(reach):
        taker = {}

        def claim(chip, seen):
            sources = list(left[chip])
            draw.shuffle(sources)
            for source in sources:
                if source not in seen:
                    seen.add(source)
                    if source not in taker or claim(taker[source], seen):
                        taker[source] = chip
                        return True
            return False

        chip_order = list(range(chips))
        draw.shuffle(chip_order)
        for chip in chip_order:
            claim(chip, set())
        matching = [0] * chips
        for source, chip in taker.items():
            matching[chip] = source
            left[chip].remove(source)
        plan.append(matching)
    return plan


def fetch_routes(chips, reach):
    if all(len(row) == 2 * chips for row in ROUTES):
        return ROUTES
    plan = fetch_plan(chips, reach, PLAN_SEED)
    if reach % 2:
        plan.append(plan[-1])
    return [
        [plan[step + side][chip] * 2 + side for chip in range(chips) for side in range(2)]
        for step in range(0, len(plan), 2)
    ]


def vmem(count):
    return [pl.BlockSpec(memory_space=pltpu.VMEM)] * count


def smem(count):
    return [pl.BlockSpec(memory_space=pltpu.SMEM)] * count


def hbm(count):
    return [pl.BlockSpec(memory_space=pltpu.HBM)] * count


def shards(file_blocks, block_target):
    slot_count, channels, samples = file_blocks.shape
    devices = lax.axis_size("chan")
    chips = devices // 2
    half_cycle = devices // 2
    reach = (half_cycle + 1) // 2
    routes = fetch_routes(chips, reach)
    steps = len(routes)
    device = lax.axis_index("chan").astype(jnp.int32).reshape(1)
    ahead = [
        [(row[2 * chip + side] // 2 - chip) % chips for chip in range(chips)]
        for row in routes
        for side in range(2)
    ]
    transform = jnp.asarray(
        np.concatenate([fourier_table(samples, BANDS, BAND_LO), sum_table(BANDS, SMOOTH)])
    )
    lag_rows = jnp.asarray(lag_table(samples, BANDS, BAND_LO, LAGS, NW))

    def swap_cores(value):
        return lax.ppermute(value, "chan", [(s, s ^ 1) for s in range(devices)])

    def fetch(value, row):
        return lax.ppermute(value, "chan", [(source, at) for at, source in enumerate(row)])

    far_target = swap_cores(block_target)
    far_blocks = swap_cores(file_blocks)
    inputs = (block_target, file_blocks, transform)
    target, blocks, table = pl.pallas_call(
        load_kernel,
        out_shape=[jax.ShapeDtypeStruct(v.shape, v.dtype) for v in inputs],
        in_specs=hbm(3),
        out_specs=vmem(3),
        scratch_shapes=[pltpu.SemaphoreType.DMA((3,))],
        compiler_params=pltpu.CompilerParams(vmem_limit_bytes=8 << 20),
        cost_estimate=pl.CostEstimate(flops=1 << 20, bytes_accessed=1 << 20, transcendentals=0),
        name="load",
    )(*[pltpu.with_memory_space_constraint(v, pltpu.HBM) for v in inputs])
    chip_blocks = pl.pallas_call(
        spectra_kernel,
        out_shape=jax.ShapeDtypeStruct((2 * NW, channels, 2 * BANDS), jnp.bfloat16),
        in_specs=vmem(5),
        out_specs=vmem(1)[0],
        scratch_shapes=[
            pltpu.SMEM(block_target.shape, jnp.int32),
            pltpu.SMEM(block_target.shape, jnp.int32),
            pltpu.SemaphoreType.DMA((2,)),
        ],
        compiler_params=pltpu.CompilerParams(vmem_limit_bytes=8 << 20),
        name="spectra",
    )(target, far_target, blocks, far_blocks, table)
    fetched = [fetch(chip_blocks, row) for row in routes]
    steer = pl.pallas_call(
        steer_kernel,
        out_shape=jax.ShapeDtypeStruct((channels, LAGS, NW * 2 * BANDS), jnp.bfloat16),
        in_specs=smem(1) + vmem(2),
        out_specs=vmem(1)[0],
        compiler_params=pltpu.CompilerParams(vmem_limit_bytes=8 << 20),
        cost_estimate=pl.CostEstimate(flops=6 << 20, bytes_accessed=2 << 20, transcendentals=0),
        name="steer",
    )(device, chip_blocks, lag_rows)
    mine, steer = lax.optimization_barrier((jnp.stack(fetched), steer))
    other = swap_cores(mine)
    columns = (half_cycle + 1) * channels
    return pl.pallas_call(
        functools.partial(product_kernel, ahead),
        out_shape=jax.ShapeDtypeStruct((channels, LAGS, columns), jnp.bfloat16),
        in_specs=smem(1) + vmem(4),
        out_specs=hbm(1)[0],
        scratch_shapes=[
            pltpu.VMEM((2 * (reach + 1), channels, NW * 2 * BANDS), jnp.bfloat16),
            pltpu.VMEM((channels, LAGS, columns), jnp.bfloat16),
            pltpu.SemaphoreType.DMA((PIECES,)),
        ],
        compiler_params=pltpu.CompilerParams(vmem_limit_bytes=32 << 20),
        name="product",
    )(device, steer, chip_blocks, mine, other)


def solution(mesh):
    return jax.shard_map(
        shards,
        mesh=mesh,
        in_specs=(P(("day", "chan"), None, None), P(("day", "chan"))),
        out_specs=P(("day", "chan"), None, None),
        check_vma=False,
    )
```

```python
import functools
import math
import random

import jax
import jax.numpy as jnp
import numpy as np
from jax import lax
from jax.experimental import pallas as pl
from jax.experimental.pallas import tpu as pltpu
from jax.sharding import PartitionSpec as P

NW = 4
BANDS = 128
BAND_LO = 16
SMOOTH = 4
LAGS = 64
PIECES = 4
PLAN_SEED = 4034
ROUTES = (
    (5, 3, 7, 11, 9, 6, 15, 8, 13, 10, 12, 0, 14, 2, 1, 4),
    (7, 9, 8, 4, 10, 13, 11, 12, 14, 0, 15, 3, 1, 5, 6, 2),
)


def fourier_table(samples, bands, band_low):
    times = np.arange(samples, dtype=np.int32)
    bins = band_low + np.arange(bands, dtype=np.int32)
    phase = times[:, None] * bins[None, :] % samples
    step = np.float32(2.0 * math.pi / samples)
    angle = step * phase.astype(np.float32)
    half = np.float32(0.5)
    taper = half - half * np.cos(step * times.astype(np.float32))
    rows = np.concatenate([taper[:, None] * np.cos(angle), -taper[:, None] * np.sin(angle)], axis=1)
    return rows.astype(jnp.bfloat16)


def lag_table(samples, bands, band_low, lags, windows):
    bins = band_low + np.arange(bands, dtype=np.int32)
    delays = np.arange(lags, dtype=np.int32) - lags // 2
    phase = bins[None, :] * delays[:, None] % samples
    angle = np.float32(2.0 * math.pi / samples) * phase.astype(np.float32)
    weight = np.float32(1.0 / math.sqrt(windows * bands))
    rows = np.stack([np.cos(angle) * weight, -np.sin(angle) * weight])
    return rows.astype(jnp.bfloat16).astype(np.float32)


def load_kernel(target_hbm, blocks_hbm, table_hbm, target_ref, blocks_ref, table_ref, sems):
    samples = table_hbm.shape[0]
    pairs = [
        (table_hbm, table_ref.at[pl.ds(0, samples)]),
        (blocks_hbm, blocks_ref),
        (target_hbm, target_ref),
    ]
    copies = [pltpu.make_async_copy(here, there, sems.at[at]) for at, (here, there) in enumerate(pairs)]
    for copy in copies:
        copy.start()
    row = lax.broadcasted_iota(jnp.int32, (BANDS, 2 * BANDS), 0)
    column = lax.broadcasted_iota(jnp.int32, (BANDS, 2 * BANDS), 1)
    near = (column >= BANDS) | (jnp.abs(row - column) <= SMOOTH)
    ones = jnp.where(near, 1.0, 0.0).astype(jnp.bfloat16)
    table_ref[samples : samples + BANDS] = ones
    table_ref[samples + BANDS :] = ones
    for copy in copies:
        copy.wait()


def spectra_kernel(
    target_ref, far_target_ref, blocks_ref, far_blocks_ref, table_ref, out_ref, target, far_target, sems
):
    slots, channels, samples = blocks_ref.shape
    places = 2 * NW
    copies = [
        pltpu.make_async_copy(target_ref, target, sems.at[0]),
        pltpu.make_async_copy(far_target_ref, far_target, sems.at[1]),
    ]
    for copy in copies:
        copy.start()
    rows = jnp.concatenate(
        [ref[...].reshape(slots * channels, samples) for ref in (blocks_ref, far_blocks_ref)]
    )
    spectra = jnp.dot(rows, table_ref[:samples], preferred_element_type=jnp.float32)
    real_part = spectra[:, :BANDS]
    imag_part = spectra[:, BANDS:]
    power = real_part * real_part + imag_part * imag_part
    high = power.astype(jnp.bfloat16)
    low = (power - high.astype(jnp.float32)).astype(jnp.bfloat16)
    sums = jnp.dot(
        jnp.concatenate([high, low], axis=1), table_ref[samples:], preferred_element_type=jnp.float32
    )
    level = sums[:, :BANDS] * (1.0 / (2 * SMOOTH + 1)) + sums[:, BANDS:] * (0.25 / BANDS) + 1e-05
    factor = lax.rsqrt(level)
    real_part = (real_part * factor).astype(jnp.bfloat16)
    imag_part = (imag_part * factor).astype(jnp.bfloat16)
    for copy in copies:
        copy.wait()
    first = lax.rem(target[0], places)
    for slot in reversed(range(2 * slots)):
        value = target[slot] if slot < slots else far_target[slot - slots]
        place = jnp.where(value >= 0, lax.rem(value, places), first)
        span = slice(slot * channels, (slot + 1) * channels)
        out_ref[place, :, :BANDS] = real_part[span]
        out_ref[place, :, BANDS:] = imag_part[span]


def steer_kernel(device_ref, chip_ref, lag_ref, out_ref):
    channels = chip_ref.shape[1]
    core = lax.rem(device_ref[0], 2)
    lag_cos = lag_ref[0]
    lag_sin = lag_ref[1]
    for window in range(NW):
        own = chip_ref[core * NW + window].astype(jnp.float32)
        low = window * 2 * BANDS
        for channel in range(channels):
            real_part = own[channel : channel + 1, :BANDS]
            imag_part = own[channel : channel + 1, BANDS:]
            first = lag_cos * real_part + lag_sin * imag_part
            second = lag_cos * imag_part - lag_sin * real_part
            out_ref[channel, :, low : low + BANDS] = first.astype(jnp.bfloat16)
            out_ref[channel, :, low + BANDS : low + 2 * BANDS] = second.astype(jnp.bfloat16)


def entry(table, index):
    bits = max(table).bit_length()
    count = 30 // bits
    word = jnp.int32(0)
    for start in range(0, len(table), count):
        packed = sum(value << bits * at for at, value in enumerate(table[start : start + count]))
        word = jnp.where(index >= start, jnp.int32(packed), word)
    shift = bits * lax.rem(index, count)
    return lax.shift_right_logical(word, shift) & ((1 << bits) - 1)


def product_kernel(
    ahead, device_ref, steer_ref, chip_ref, mine_ref, other_ref, out_hbm, gathered, out_ref, sems
):
    channels, lags, columns = out_ref.shape
    offsets = columns // channels
    width = 2 * BANDS
    device = device_ref[0]
    core = lax.rem(device, 2)
    own_chip = lax.div(device, 2)

    def place(chip, blocks):
        for owner in range(2):
            for window in range(NW):
                gathered[2 * chip + owner, :, window * width : (window + 1) * width] = blocks[
                    owner * NW + window
                ]

    place(0, chip_ref)
    for step in range(mine_ref.shape[0]):
        even = entry(ahead[2 * step], own_chip)
        odd = entry(ahead[2 * step + 1], own_chip)
        place(jnp.where(core == 0, even, odd), mine_ref.at[step])
        place(jnp.where(core == 0, odd, even), other_ref.at[step])
    right = gathered[pl.ds(core, offsets)].reshape(columns, NW * width)
    left = steer_ref[...].reshape(channels * lags, NW * width)
    total = lax.dot_general(
        left, right, (((1,), (1,)), ((), ())), preferred_element_type=jnp.float32
    )
    count = channels // PIECES
    copies = []
    for piece in range(PIECES):
        span = slice(piece * count * lags, (piece + 1) * count * lags)
        part = slice(piece * count, (piece + 1) * count)
        out_ref[part] = total[span].astype(jnp.bfloat16).reshape(count, lags, columns)
        copies.append(pltpu.make_async_copy(out_ref.at[part], out_hbm.at[part], sems.at[piece]))
        copies[-1].start()
    for copy in copies:
        copy.wait()


def fetch_plan(chips, reach, seed):
    draw = random.Random(seed)
    left = [[(chip + offset) % chips for offset in range(1, reach + 1)] for chip in range(chips)]
    plan = []
    for _ in range(reach):
        taker = {}

        def claim(chip, seen):
            sources = list(left[chip])
            draw.shuffle(sources)
            for source in sources:
                if source not in seen:
                    seen.add(source)
                    if source not in taker or claim(taker[source], seen):
                        taker[source] = chip
                        return True
            return False

        chip_order = list(range(chips))
        draw.shuffle(chip_order)
        for chip in chip_order:
            claim(chip, set())
        matching = [0] * chips
        for source, chip in taker.items():
            matching[chip] = source
            left[chip].remove(source)
        plan.append(matching)
    return plan


def fetch_routes(chips, reach):
    if all(len(row) == 2 * chips for row in ROUTES):
        return ROUTES
    plan = fetch_plan(chips, reach, PLAN_SEED)
    if reach % 2:
        plan.append(plan[-1])
    return [
        [plan[step + side][chip] * 2 + side for chip in range(chips) for side in range(2)]
        for step in range(0, len(plan), 2)
    ]


def vmem(count):
    return [pl.BlockSpec(memory_space=pltpu.VMEM)] * count


def smem(count):
    return [pl.BlockSpec(memory_space=pltpu.SMEM)] * count


def hbm(count):
    return [pl.BlockSpec(memory_space=pltpu.HBM)] * count


def shards(file_blocks, block_target):
    slot_count, channels, samples = file_blocks.shape
    devices = lax.axis_size("chan")
    chips = devices // 2
    half_cycle = devices // 2
    reach = (half_cycle + 1) // 2
    routes = fetch_routes(chips, reach)
    steps = len(routes)
    device = lax.axis_index("chan").astype(jnp.int32).reshape(1)
    ahead = [
        [(row[2 * chip + side] // 2 - chip) % chips for chip in range(chips)]
        for row in routes
        for side in range(2)
    ]
    transform = jnp.asarray(fourier_table(samples, BANDS, BAND_LO))
    lag_rows = jnp.asarray(lag_table(samples, BANDS, BAND_LO, LAGS, NW))

    def swap_cores(value):
        return lax.ppermute(value, "chan", [(s, s ^ 1) for s in range(devices)])

    def fetch(value, row):
        return lax.ppermute(value, "chan", [(source, at) for at, source in enumerate(row)])

    far_target = swap_cores(block_target)
    far_blocks = swap_cores(file_blocks)
    inputs = (block_target, file_blocks, transform)
    target, blocks, table = pl.pallas_call(
        load_kernel,
        out_shape=[
            jax.ShapeDtypeStruct(block_target.shape, block_target.dtype),
            jax.ShapeDtypeStruct(file_blocks.shape, file_blocks.dtype),
            jax.ShapeDtypeStruct((samples + 2 * BANDS, 2 * BANDS), transform.dtype),
        ],
        in_specs=hbm(3),
        out_specs=vmem(3),
        scratch_shapes=[pltpu.SemaphoreType.DMA((3,))],
        compiler_params=pltpu.CompilerParams(vmem_limit_bytes=8 << 20),
        cost_estimate=pl.CostEstimate(flops=1 << 20, bytes_accessed=1 << 20, transcendentals=0),
        name="load",
    )(*[pltpu.with_memory_space_constraint(v, pltpu.HBM) for v in inputs])
    chip_blocks = pl.pallas_call(
        spectra_kernel,
        out_shape=jax.ShapeDtypeStruct((2 * NW, channels, 2 * BANDS), jnp.bfloat16),
        in_specs=vmem(5),
        out_specs=vmem(1)[0],
        scratch_shapes=[
            pltpu.SMEM(block_target.shape, jnp.int32),
            pltpu.SMEM(block_target.shape, jnp.int32),
            pltpu.SemaphoreType.DMA((2,)),
        ],
        compiler_params=pltpu.CompilerParams(vmem_limit_bytes=8 << 20),
        name="spectra",
    )(target, far_target, blocks, far_blocks, table)
    fetched = [fetch(chip_blocks, row) for row in routes]
    steer = pl.pallas_call(
        steer_kernel,
        out_shape=jax.ShapeDtypeStruct((channels, LAGS, NW * 2 * BANDS), jnp.bfloat16),
        in_specs=smem(1) + vmem(2),
        out_specs=vmem(1)[0],
        compiler_params=pltpu.CompilerParams(vmem_limit_bytes=8 << 20),
        cost_estimate=pl.CostEstimate(flops=6 << 20, bytes_accessed=2 << 20, transcendentals=0),
        name="steer",
    )(device, chip_blocks, lag_rows)
    mine, steer = lax.optimization_barrier((jnp.stack(fetched), steer))
    other = swap_cores(mine)
    columns = (half_cycle + 1) * channels
    return pl.pallas_call(
        functools.partial(product_kernel, ahead),
        out_shape=jax.ShapeDtypeStruct((channels, LAGS, columns), jnp.bfloat16),
        in_specs=smem(1) + vmem(4),
        out_specs=hbm(1)[0],
        scratch_shapes=[
            pltpu.VMEM((2 * (reach + 1), channels, NW * 2 * BANDS), jnp.bfloat16),
            pltpu.VMEM((channels, LAGS, columns), jnp.bfloat16),
            pltpu.SemaphoreType.DMA((PIECES,)),
        ],
        compiler_params=pltpu.CompilerParams(vmem_limit_bytes=32 << 20),
        name="product",
    )(device, steer, chip_blocks, mine, other)


def solution(mesh):
    return jax.shard_map(
        shards,
        mesh=mesh,
        in_specs=(P(("day", "chan"), None, None), P(("day", "chan"))),
        out_specs=P(("day", "chan"), None, None),
        check_vma=False,
    )
```
